256 devices in a mesh: dp: 2 (over core), ctx: 32 (over z, x), mp: 4 (over y).
Axes of the slice: x: 4, y: 4, z: 8, core: 2. Of those that a mesh axis runs over, the one named last changes fastest.
Arguments:
- image_states: bfloat16 [2, 8192, 8192], P('dp', 'ctx', 'mp'), may hold values from -6 to 6
- place_index: int32 [2, 8192], P('dp'), may hold values from 0 to 16383, as said below
- doc_ids: int32 [2, 16384], P('dp'), may hold values from 0 to 127, never falling along the last dimension, each value on 1 to 512 neighbouring positions
- queries: bfloat16 [2, 16384, 4096], P('dp', 'ctx', 'mp'), may hold values from -160 to 160
- text_kv: bfloat16 [2, 16384, 1024], P('dp', 'ctx', 'mp'), may hold values from -5.5 to 5.5
- kv_weight: bfloat16 [4, 8192, 256], P('mp'), may hold values from -0.0625 to 0.0625
- d_out: bfloat16 [2, 16384, 4096], P('dp', 'ctx', 'mp'), may hold values from -6 to 6
Outputs:
- attn_out: bfloat16 [2, 16384, 4096], P('dp', 'ctx', 'mp')
- image_grad: bfloat16 [2, 8192, 8192], P('dp', 'ctx', 'mp')
- kv_weight_grad: float32 [4, 8192, 256], P('mp', 'ctx')
The draws below stay inside these ranges and needn't reach their ends.
Inputs may be any that keep to these rules, and one draw needn't show every extreme that they name: `place_index`: images are whole blocks of 16 image tokens, consecutive in a vision rank's order and placed on 16 consecutive positions aligned to 16; every context shard of 512 positions holds exactly 256 image tokens; no position gets two image tokens; at most 16 image tokens of one vision rank lie in one context shard, and in every draw some vision rank places exactly 16 in some shard.
All inputs are finite; a program needn't handle non-finite values.
Results may differ from the reference program's by a relative error of at most 0.0085.
Values may be sent and summed in bfloat16 or wider, within the bound.
A program may use at most 128 MiB of HBM per device.

```python
import math
import jax
import jax.numpy as jnp
import numpy as np
from jax import lax

D = 8192
HD = 128
KV_HEADS = 4
GROUP = 8
QH = 32
CTX_DEV = 512
IMGTOK = 16
IMG_DEV = 256
LEN = 16384
NIMG = 8192
DOCS = 128
N_DP = 2
N_CTX = 32


def image_layout(key):
    per_rank = IMG_DEV // IMGTOK
    blocks = CTX_DEV // IMGTOK

    def one_replica(replica_key):
        perm_key, slot_key = jax.random.split(replica_key)
        offsets = jax.random.permutation(perm_key, N_CTX).astype(jnp.int32)
        half_way = N_CTX // 2
        first_offset = offsets[0]
        slot_ids = jnp.arange(N_CTX, dtype=jnp.int32)
        offsets = jnp.where(offsets == half_way, first_offset, offsets)
        offsets = jnp.where(slot_ids == 0, half_way, offsets).astype(jnp.int32)
        rank_ids = jnp.arange(N_CTX, dtype=jnp.int32)[:, None]
        images = jnp.arange(per_rank, dtype=jnp.int32)[None, :]
        target = (rank_ids + offsets[images % N_CTX]) % N_CTX
        scores = jax.random.randint(slot_key, (N_CTX, blocks), 0, 1 << 20) * blocks + jnp.arange(blocks, dtype=jnp.int32)[None, :]
        block_order = jnp.argsort(scores, axis=1).astype(jnp.int32)
        chosen_block = block_order[target, jnp.broadcast_to(images, target.shape)]
        starts = target * CTX_DEV + chosen_block * IMGTOK
        positions = starts[:, :, None] + jnp.arange(IMGTOK, dtype=jnp.int32)[None, None, :]
        return positions.reshape(NIMG).astype(jnp.int32)
    return jax.vmap(one_replica)(jax.random.split(key, N_DP))


def attention_inputs(key):
    query_key = jax.random.fold_in(key, 11)
    value_key = jax.random.fold_in(key, 13)
    query_vals = jnp.clip(jax.random.normal(query_key, (N_DP, LEN, QH * HD), jnp.float32), -5.5, 5.5)
    key_values = jnp.clip(jax.random.normal(value_key, (N_DP, LEN, KV_HEADS * 2 * HD), jnp.float32), -5.5, 5.5)
    return (query_vals, key_values)


def draw_place_index(key, part):
    return image_layout(jax.random.fold_in(key, 7))


def draw_queries(key, part):
    return attention_inputs(key)[0].astype(jnp.bfloat16)


def draw_text_kv(key, part):
    return attention_inputs(key)[1].astype(jnp.bfloat16)


def level_of(own_key, extent, shards, low, largest):
    gain = 1.0
    for dim, shards_of in shards:
        draws = jax.random.uniform(jax.random.fold_in(jax.random.fold_in(own_key, 6), dim), (shards_of,), jnp.float32, low / len(shards), largest / len(shards))
        gain = gain * jnp.repeat(jnp.exp(draws), extent[dim] // shards_of).reshape((-1,) + (1,) * (len(extent) - 1 - dim))
    return gain


def length_profile(amount, total, most, slope):
    portions = [(1 << 20) // math.isqrt(rank ** slope) + 1 for rank in range(2, amount + 1)]
    rest, counts = total - most - (amount - 1), [1] * (amount - 1)
    while rest > 0:
        candidates = [i for i in range(amount - 1) if counts[i] < most]
        whole, remaining = sum([portions[i] for i in candidates]), rest
        for i in candidates:
            extra = min(most - counts[i], max(1, remaining * portions[i] // whole), rest)
            counts[i] = counts[i] + extra
            rest = rest - extra
    return np.array([most] + counts)


def uneven(own_key, count, total, most, slope):
    if count == 2:
        one = jax.random.randint(own_key, (), max(1, total - most), min(most, total - 1) + 1)
        return jnp.stack([one, total - one])
    tallies = jnp.asarray(length_profile(count, total, most, slope), jnp.int32)
    twos = (count - 1) // 2
    donor, receiver = tallies[1:1 + 2 * twos:2], tallies[2:2 + 2 * twos:2]
    slack = jnp.minimum(donor - 1, most - receiver)
    passed = jax.random.randint(jax.random.fold_in(own_key, 1), (twos,), 0, 1 << 20) % (slack + 1)
    tallies = tallies.at[1:1 + 2 * twos:2].set(donor - passed).at[2:2 + 2 * twos:2].set(receiver + passed)
    return tallies[jax.random.permutation(jax.random.fold_in(own_key, 2), count)]


def noise(rng, extent, spread, bound, cuts=(), kind=jnp.bfloat16):
    gain = level_of(rng, extent, cuts, -0.22, 0.18) if cuts else 1.0
    result = jax.random.normal(rng, extent, jnp.float32) * spread * gain
    return jnp.minimum(jnp.maximum(result, -bound), bound).astype(kind)


def setup_inputs(seed: int = 0) -> dict:
    keys = jax.random.split(jax.random.key(seed), 8)
    return {
        "image_states": noise(keys[0], (N_DP, NIMG, D), 1.0, 6.0, ((0, 2), (1, 32), (2, 4))),
        "place_index": draw_place_index(jax.random.fold_in(keys[7], 71), 0),
        "doc_ids": jax.vmap(lambda own: jnp.searchsorted(jnp.cumsum(uneven(own, DOCS, LEN, CTX_DEV, 2)), jnp.arange(LEN), side="right"))(jax.random.split(keys[2], N_DP)).reshape((N_DP, LEN)).astype(jnp.int32),
        "queries": draw_queries(jax.random.fold_in(keys[7], 71), 0),
        "text_kv": draw_text_kv(jax.random.fold_in(keys[7], 71), 0),
        "kv_weight": noise(keys[5], (KV_HEADS, D, 2 * HD), D ** -0.5, 0.0625, ((0, 4),)),
        "d_out": noise(keys[6], (N_DP, LEN, QH * HD), 1.0, 6.0, ((0, 2), (1, 32), (2, 4))),
    }


def shard_pass(query_rows, grad_rows, key_window, key_docs, own_docs):
    score_scale = HD ** -0.5
    query_all = query_rows.reshape(CTX_DEV, KV_HEADS, GROUP, HD).astype(jnp.float32)
    grad_all = grad_rows.reshape(CTX_DEV, KV_HEADS, GROUP, HD).astype(jnp.float32)
    parted = key_window.reshape(2 * CTX_DEV, KV_HEADS, 2, HD).astype(jnp.float32)
    key_part = parted[:, :, 0, :]
    value_part = parted[:, :, 1, :]
    query_pos = jnp.arange(CTX_DEV, dtype=jnp.int32)
    key_pos = jnp.arange(2 * CTX_DEV, dtype=jnp.int32) - CTX_DEV
    allowed = (key_pos[None, :] <= query_pos[:, None]) & (key_docs[None, :] == own_docs[:, None])
    scores = jnp.einsum('qhgd,khd->hgqk', query_all, key_part) * score_scale
    scores = jnp.where(allowed[None, None], scores, -1e30)
    shifted = jnp.exp(scores - jnp.max(scores, axis=3, keepdims=True))
    shifted = jnp.where(allowed[None, None], shifted, 0.0)
    attention = shifted / jnp.sum(shifted, axis=3, keepdims=True)
    attention_low = lax.optimization_barrier(attention.astype(jnp.bfloat16)).astype(jnp.float32)
    context = jnp.einsum('hgqk,khd->qhgd', attention_low, value_part)
    grad_attention = jnp.einsum('qhgd,khd->hgqk', grad_all, value_part)
    row_delta = jnp.einsum('qhgd,qhgd->hgq', grad_all, context)[..., None]
    grad_scores = attention * (grad_attention - row_delta)
    grad_scores = lax.optimization_barrier(grad_scores.astype(jnp.bfloat16)).astype(jnp.float32)
    key_grad = score_scale * jnp.einsum('hgqk,qhgd->khd', grad_scores, query_all)
    value_grad = jnp.einsum('hgqk,qhgd->khd', attention_low, grad_all)
    kv_grad = jnp.stack([key_grad, value_grad], axis=2).reshape(2 * CTX_DEV, KV_HEADS * 2 * HD)
    return context.astype(jnp.bfloat16).reshape(CTX_DEV, QH * HD), kv_grad


def reference(image_states, place_index, doc_ids, queries, text_kv, kv_weight, d_out):
    heads_weight = kv_weight.transpose(1, 0, 2).reshape(D, KV_HEADS * 2 * HD)
    flat_states = image_states.reshape(N_DP * NIMG, D)
    image_kv = jnp.dot(flat_states, heads_weight, preferred_element_type=jnp.float32).astype(jnp.bfloat16)
    image_kv = image_kv.reshape(N_DP, NIMG, KV_HEADS * 2 * HD)
    out_list = []
    grad_list = []
    for replica in range(N_DP):
        kv_full = text_kv[replica].at[place_index[replica]].set(image_kv[replica])
        padded_kv = jnp.concatenate([jnp.zeros((CTX_DEV, KV_HEADS * 2 * HD), jnp.bfloat16), kv_full], axis=0)
        padded_docs = jnp.concatenate([jnp.full((CTX_DEV,), -1, jnp.int32), doc_ids[replica]], axis=0)
        replica_queries = queries[replica]
        replica_grads = d_out[replica]
        replica_docs = doc_ids[replica]

        def one_shard(running_sums, shard_index):
            first_row = shard_index * CTX_DEV
            key_window = lax.dynamic_slice_in_dim(padded_kv, first_row, 2 * CTX_DEV)
            key_docs = lax.dynamic_slice_in_dim(padded_docs, first_row, 2 * CTX_DEV)
            own_docs = lax.dynamic_slice_in_dim(replica_docs, first_row, CTX_DEV)
            query_rows = lax.dynamic_slice_in_dim(replica_queries, first_row, CTX_DEV)
            grad_rows = lax.dynamic_slice_in_dim(replica_grads, first_row, CTX_DEV)
            output, kv_grad = shard_pass(query_rows, grad_rows, key_window, key_docs, own_docs)
            current = lax.dynamic_slice_in_dim(running_sums, first_row, 2 * CTX_DEV)
            running_sums = lax.dynamic_update_slice_in_dim(running_sums, current + kv_grad, first_row, 0)
            return running_sums, output

        initial = jnp.zeros(((N_CTX + 1) * CTX_DEV, KV_HEADS * 2 * HD), jnp.float32)
        grad_padded, outputs = lax.scan(one_shard, initial, jnp.arange(N_CTX, dtype=jnp.int32))
        out_list.append(outputs.reshape(LEN, QH * HD))
        grad_list.append(grad_padded[CTX_DEV:][place_index[replica]].astype(jnp.bfloat16))
    attn_out = jnp.stack(out_list)
    flat_grad = jnp.stack(grad_list).reshape(N_DP * NIMG, KV_HEADS * 2 * HD)
    image_grad = lax.dot_general(flat_grad, heads_weight, (((1,), (1,)), ((), ())), preferred_element_type=jnp.float32)
    image_grad = image_grad.astype(jnp.bfloat16).reshape(N_DP, NIMG, D)
    weight_flat = lax.dot_general(flat_states, flat_grad, (((0,), (0,)), ((), ())), preferred_element_type=jnp.float32)
    kv_weight_grad = weight_flat.reshape(D, KV_HEADS, 2 * HD).transpose(1, 0, 2)
    return attn_out, image_grad, kv_weight_grad
```

```python
import functools
import math

import jax
import jax.numpy as jnp
from jax import lax
from jax.experimental import pallas as pl
from jax.experimental.pallas import tpu as pltpu
from jax.sharding import PartitionSpec as P

IMGTOK = 16
BF16 = jnp.bfloat16
F32 = jnp.float32
MESH = pl.DeviceIdType.MESH


def dot_nn(a, b):
    return jnp.dot(a, b, preferred_element_type=F32)


def dot_nt(a, b):
    return lax.dot_general(a, b, (((1,), (1,)), ((), ())), preferred_element_type=F32)


def iota(shape, dim):
    return lax.broadcasted_iota(jnp.int32, shape, dim)


def ring_order(count):
    return sorted(range(count), key=lambda k: (min(k, count - k), k))


def remote(src, dst, send_sem, recv_sem, device):
    return pltpu.make_async_remote_copy(
        src_ref=src,
        dst_ref=dst,
        send_sem=send_sem,
        recv_sem=recv_sem,
        device_id=device,
        device_id_type=MESH,
    )


def slot_exchange(packed, arrived, send_sems, recv_sems, c, n):
    def copy_of(k):
        p = lax.rem(c + k, n)
        return remote(
            packed.at[pl.ds(pl.multiple_of(p * IMGTOK, IMGTOK), IMGTOK)],
            arrived.at[pl.ds(pl.multiple_of(c * IMGTOK, IMGTOK), IMGTOK)],
            send_sems.at[k],
            recv_sems.at[k],
            {"ctx": p},
        )

    def start(k, carry):
        copy_of(k).start()
        return carry

    def finish(k, carry):
        copy_of(k).wait()
        return carry

    lax.fori_loop(1, n, start, 0)
    mine = pl.ds(pl.multiple_of(c * IMGTOK, IMGTOK), IMGTOK)
    arrived[mine, :] = packed[mine, :]
    lax.fori_loop(1, n, finish, 0)


def route_kernel(
    n,
    mp,
    slot_row,
    pos_row,
    text,
    states,
    weights,
    own_out,
    prev_out,
    wh_out,
    sht_out,
    sh,
    wh,
    sht,
    psend,
    precv,
    acc,
    yrecv,
    packed,
    arrived,
    own_kv,
    prev_kv,
    local_sems,
    s_sems,
    w_send,
    w_recv,
    p_send,
    p_recv,
    y_send,
    y_recv,
    a_send,
    a_recv,
    k_sems,
):
    c = lax.axis_index("ctx")
    m = lax.axis_index("mp")
    d = lax.axis_index("dp")
    half = sh.shape[2]
    tokens = sh.shape[1]
    order = ring_order(mp)

    get_w = pltpu.make_async_copy(
        weights.at[pl.ds(pl.multiple_of(m * 2 * half + d * half, half), half)],
        wh.at[m],
        local_sems.at[0],
    )
    get_s = pltpu.make_async_copy(
        states.at[:, pl.ds(pl.multiple_of(d * half, half), half)], sh.at[d], local_sems.at[1]
    )
    get_w.start()
    get_s.start()

    barrier = pltpu.get_barrier_semaphore()
    pl.semaphore_signal(barrier, inc=1, device_id={"dp": 1 - d}, device_id_type=MESH)
    for k in range(1, mp):
        pl.semaphore_signal(
            barrier, inc=1, device_id={"mp": lax.rem(m + k, mp)}, device_id_type=MESH
        )

    def greet(k, carry):
        pl.semaphore_signal(
            barrier, inc=1, device_id={"ctx": lax.rem(c + k, n)}, device_id_type=MESH
        )
        return carry

    lax.fori_loop(1, n, greet, 0)
    pl.semaphore_wait(barrier, 1 + (mp - 1) + (n - 1))

    w_copies = {}
    for k in reversed(order):
        if k:
            p = lax.rem(m + k, mp)
            w_copies[k] = remote(
                weights.at[pl.ds(pl.multiple_of(p * 2 * half + d * half, half), half)],
                wh.at[m],
                w_send.at[k],
                w_recv.at[k],
                {"mp": p},
            )
            w_copies[k].start()
    s_copy = remote(
        states.at[:, pl.ds(pl.multiple_of((1 - d) * half, half), half)],
        sh.at[d],
        s_sems.at[0],
        s_sems.at[1],
        {"dp": 1 - d},
    )
    s_copy.start()
    get_s.wait()
    get_w.wait()
    s_copy.wait()
    for b in range(2):
        sht[:, b * tokens : (b + 1) * tokens] = sh[b].T
    put_sht = pltpu.make_async_copy(sht, sht_out, local_sems.at[2])
    put_sht.start()

    p_copies = {}
    for k in order:
        h = lax.rem(m - k + mp, mp)
        if k:
            w_copies[k].wait_recv()
        psend[k] = dot_nn(sh[1 - d], wh[h])
        p_copies[k] = remote(
            psend.at[k], precv.at[k], p_send.at[k], p_recv.at[k], {"dp": 1 - d}
        )
        p_copies[k].start()
        acc[k] = dot_nn(sh[d], wh[h])
    put_wh = pltpu.make_async_copy(wh, wh_out, local_sems.at[3])
    put_wh.start()

    y_copies = {}
    for k in reversed(order):
        p_copies[k].wait_recv()
        acc[k] = acc[k] + precv[k]
        if k:
            y_copies[k] = remote(
                acc.at[k],
                yrecv.at[k],
                y_send.at[k],
                y_recv.at[k],
                {"mp": lax.rem(m - k + mp, mp)},
            )
            y_copies[k].start()
    total = acc[0]
    for k in order:
        if k:
            y_copies[k].wait_recv()
            total = total + yrecv[k]
    image_kv = total.astype(BF16)

    pick = (iota((n * IMGTOK, tokens), 0) == slot_row[...]).astype(F32).astype(BF16)
    packed[...] = dot_nn(pick, image_kv).astype(BF16)
    slot_exchange(packed, arrived, a_send, a_recv, c, n)

    place = (iota((text.shape[0], n * IMGTOK), 0) == pos_row[...]).astype(F32)
    is_image = jnp.sum(place, axis=1, keepdims=True) > 0.5
    placed = dot_nn(place.astype(BF16), arrived[...])
    own_kv[...] = jnp.where(is_image, placed, text[...].astype(F32)).astype(BF16)
    shift = remote(
        own_kv, prev_kv, k_sems.at[0], k_sems.at[1], {"ctx": lax.rem(c + 1, n)}
    )
    shift.start()
    put_own = pltpu.make_async_copy(own_kv, own_out, local_sems.at[4])
    put_own.start()
    shift.wait()
    put_prev = pltpu.make_async_copy(prev_kv, prev_out, local_sems.at[5])
    put_prev.start()

    for k in range(mp):
        p_copies[k].wait_send()
        if k:
            w_copies[k].wait_send()
            y_copies[k].wait_send()
    put_sht.wait()
    put_wh.wait()
    put_own.wait()
    put_prev.wait()


def route(slot_row, pos_row, text, states, weights, n, mp):
    tokens, slice_width = states.shape
    half = slice_width // 2
    width = weights.shape[1]
    ctx_dev = text.shape[0]
    slots = n * IMGTOK
    vmem = pl.BlockSpec(memory_space=pltpu.VMEM)
    hbm = pl.BlockSpec(memory_space=pl.ANY)
    dma = pltpu.SemaphoreType.DMA
    return pl.pallas_call(
        functools.partial(route_kernel, n, mp),
        out_shape=(
            jax.ShapeDtypeStruct((ctx_dev, width), BF16),
            jax.ShapeDtypeStruct((ctx_dev, width), BF16),
            jax.ShapeDtypeStruct((mp, half, width), BF16),
            jax.ShapeDtypeStruct((half, 2 * tokens), BF16),
        ),
        in_specs=[vmem, vmem, vmem, hbm, hbm],
        out_specs=(hbm, hbm, hbm, hbm),
        scratch_shapes=[
            pltpu.VMEM((2, tokens, half), BF16),
            pltpu.VMEM((mp, half, width), BF16),
            pltpu.VMEM((half, 2 * tokens), BF16),
            pltpu.VMEM((mp, tokens, width), F32),
            pltpu.VMEM((mp, tokens, width), F32),
            pltpu.VMEM((mp, tokens, width), F32),
            pltpu.VMEM((mp, tokens, width), F32),
            pltpu.VMEM((slots, width), BF16),
            pltpu.VMEM((slots, width), BF16),
            pltpu.VMEM((ctx_dev, width), BF16),
            pltpu.VMEM((ctx_dev, width), BF16),
            dma((6,)),
            dma((2,)),
            dma((mp,)),
            dma((mp,)),
            dma((mp,)),
            dma((mp,)),
            dma((mp,)),
            dma((mp,)),
            dma((n,)),
            dma((n,)),
            dma((2,)),
        ],
        compiler_params=pltpu.CompilerParams(
            collective_id=0, has_side_effects=True, vmem_limit_bytes=40 << 20
        ),
        name="route",
    )(slot_row, pos_row, text, states, weights)


def attention_kernel(
    block,
    q_docs,
    k_docs,
    q_ref,
    g_ref,
    prev,
    own,
    out,
    prev_grad,
    own_grad,
    bias,
    keys,
    vals,
    vals_t,
    key_sum,
    val_sum,
):
    step = pl.program_id(0)
    size, hd = q_ref.shape
    span = size + block
    scale = hd ** (-0.5)
    to_log2 = scale / math.log(2.0)

    @pl.when(step == 0)
    def _():
        keys[:size] = prev[:, :hd]
        keys[size:] = own[:, :hd]
        vals[:size] = prev[:, hd:]
        vals[size:] = own[:, hd:]
        vals_t[...] = vals[...].T
        key_sum[...] = jnp.zeros_like(key_sum)
        val_sum[...] = jnp.zeros_like(val_sum)
        for i in range(size // block):
            first = i * block
            key_pos = iota((span, block), 0) + (first - size)
            query_pos = iota((span, block), 1) + first
            allowed = (key_pos <= query_pos) & (
                k_docs[first : first + span, :] == q_docs[:, first : first + block]
            )
            bias[i] = jnp.where(allowed, 0.0, -1e30)

    for i in range(size // block):
        first = i * block
        rows = slice(first, first + block)
        window = slice(first, first + span)
        q = q_ref[rows, :]
        g = g_ref[rows, :]
        scores = dot_nt(keys[window, :], q) * to_log2 + bias[i]
        shifted = jnp.exp2(scores - jnp.max(scores, axis=0, keepdims=True))
        probs = shifted * (1.0 / jnp.sum(shifted, axis=0, keepdims=True))
        low = probs.astype(BF16)
        context = dot_nn(vals_t[:, window], low)
        grad_probs = dot_nt(vals[window, :], g)
        delta = jnp.sum(g.T.astype(F32) * context, axis=0, keepdims=True)
        grad_scores = (probs * (grad_probs - delta)).astype(BF16)
        out[rows, :] = context.T.astype(BF16)
        key_sum[window, :] += dot_nn(grad_scores, q)
        val_sum[window, :] += dot_nn(low, g)

    @pl.when(step == pl.num_programs(0) - 1)
    def _():
        prev_grad[:, :hd] = (key_sum[:size] * scale).astype(BF16)
        prev_grad[:, hd:] = val_sum[:size].astype(BF16)
        own_grad[:, :hd] = key_sum[size:] * scale
        own_grad[:, hd:] = val_sum[size:]


def attention(q_docs, k_docs, queries, grads, prev, own, hd):
    size, width = queries.shape
    block = size // 2
    fixed = lambda g: (0, 0)
    by_head = lambda g: (0, g)
    return pl.pallas_call(
        functools.partial(attention_kernel, block),
        grid=(width // hd,),
        out_shape=(
            jax.ShapeDtypeStruct((size, width), BF16),
            jax.ShapeDtypeStruct((size, 2 * hd), BF16),
            jax.ShapeDtypeStruct((size, 2 * hd), F32),
        ),
        in_specs=[
            pl.BlockSpec((1, size), fixed),
            pl.BlockSpec((2 * size, 1), fixed),
            pl.BlockSpec((size, hd), by_head),
            pl.BlockSpec((size, hd), by_head),
            pl.BlockSpec((size, 2 * hd), fixed),
            pl.BlockSpec((size, 2 * hd), fixed),
        ],
        out_specs=(
            pl.BlockSpec((size, hd), by_head),
            pl.BlockSpec((size, 2 * hd), fixed),
            pl.BlockSpec((size, 2 * hd), fixed),
        ),
        scratch_shapes=[
            pltpu.VMEM((2, size + block, block), F32),
            pltpu.VMEM((2 * size, hd), BF16),
            pltpu.VMEM((2 * size, hd), BF16),
            pltpu.VMEM((hd, 2 * size), BF16),
            pltpu.VMEM((2 * size, hd), F32),
            pltpu.VMEM((2 * size, hd), F32),
        ],
        compiler_params=pltpu.CompilerParams(
            dimension_semantics=("arbitrary",), vmem_limit_bytes=48 << 20
        ),
        name="attention",
    )(q_docs, k_docs, queries, grads, prev, own)


def grad_kernel(
    n,
    mp,
    nx,
    nz,
    pos_col,
    slot_col,
    prev_grad,
    own_grad,
    wh,
    sht,
    image_out,
    weight_out,
    later,
    packed,
    arrived,
    gall,
    xs,
    xr,
    ys,
    yr,
    zr,
    wg_send,
    wg_recv,
    ig_send,
    ig_recv,
    k_sems,
    a_send,
    a_recv,
    f_send,
    f_recv,
    g_send,
    g_recv,
    x_send,
    x_recv,
    y_send,
    y_recv,
    z_send,
    z_recv,
    o_sems,
):
    c = lax.axis_index("ctx")
    m = lax.axis_index("mp")
    d = lax.axis_index("dp")
    z = c // nx
    x = lax.rem(c, nx)
    order = ring_order(mp)
    size = own_grad.shape[0]
    tokens = slot_col.shape[0]
    half = wh.shape[1]
    chunk = half // nx
    part = chunk // 2
    slots = n * IMGTOK

    barrier = pltpu.get_barrier_semaphore()
    pl.semaphore_signal(barrier, inc=1, device_id={"dp": 1 - d}, device_id_type=MESH)
    for k in range(1, mp):
        pl.semaphore_signal(
            barrier, inc=1, device_id={"mp": lax.rem(m + k, mp)}, device_id_type=MESH
        )

    def greet(k, carry):
        pl.semaphore_signal(
            barrier, inc=1, device_id={"ctx": lax.rem(c + k, n)}, device_id_type=MESH
        )
        return carry

    def greet_other(k, carry):
        pl.semaphore_signal(
            barrier,
            inc=1,
            device_id={"dp": 1 - d, "ctx": lax.rem(z + k, nz) * nx + x},
            device_id_type=MESH,
        )
        return carry

    lax.fori_loop(1, n, greet, 0)
    lax.fori_loop(1, nz, greet_other, 0)
    pl.semaphore_wait(barrier, 1 + (mp - 1) + (n - 1) + (nz - 1))

    shift = remote(
        prev_grad, later, k_sems.at[0], k_sems.at[1], {"ctx": lax.rem(c + n - 1, n)}
    )
    shift.start()
    spread = (pos_col[...] == iota((slots, size), 1)).astype(F32).astype(BF16)
    collect = (slot_col[...] == iota((tokens, slots), 1)).astype(F32).astype(BF16)
    shift.wait()
    grad_low = (own_grad[...] + later[...].astype(F32)).astype(BF16)
    packed[...] = dot_nn(spread, grad_low).astype(BF16)
    slot_exchange(packed, arrived, a_send, a_recv, c, n)
    gall[d, m] = dot_nn(collect, arrived[...]).astype(BF16)

    def to_partner(k):
        h = lax.rem(m - k + mp, mp)
        return remote(
            gall.at[d, h], gall.at[d, h], f_send.at[k], f_recv.at[k], {"dp": 1 - d}
        )

    g_copies = {}
    to_partner(0).start()
    for k in order:
        if k:
            g_copies[k] = remote(
                gall.at[d, m],
                gall.at[d, m],
                g_send.at[k],
                g_recv.at[k],
                {"mp": lax.rem(m + k, mp)},
            )
            g_copies[k].start()

    def x_copy(k, kx):
        to = lax.rem(x + kx, nx)
        return remote(
            xs.at[k, to], xr.at[k, kx], x_send.at[k, kx], x_recv.at[k, kx], {"ctx": z * nx + to}
        )

    for k in order:
        h = lax.rem(m - k + mp, mp)
        if k:
            g_copies[k].wait_recv()
            to_partner(k).start()
        to_partner(k).wait_recv()
        for j in range(nx):
            rows = slice(j * chunk, (j + 1) * chunk)
            xs[k, j] = (
                dot_nn(sht[rows, :tokens], gall[0, h]) + dot_nn(sht[rows, tokens:], gall[1, h])
            ).astype(BF16)
        for kx in range(1, nx):
            x_copy(k, kx).start()

    ig = dot_nt(gall[1 - d, 0], wh[0])
    for h in range(1, mp):
        ig = ig + dot_nt(gall[1 - d, h], wh[h])
    ig_send[...] = ig.astype(BF16)
    ig_copy = remote(ig_send, ig_recv, o_sems.at[0], o_sems.at[1], {"dp": 1 - d})
    ig_copy.start()
    ig = dot_nt(gall[d, 0], wh[0])
    for h in range(1, mp):
        ig = ig + dot_nt(gall[d, h], wh[h])
    image_out[:, pl.ds(pl.multiple_of(d * half, half), half)] = ig.astype(BF16)

    def y_copy(k):
        return remote(
            ys.at[k], yr.at[k], y_send.at[k], y_recv.at[k], {"mp": lax.rem(m - k + mp, mp)}
        )

    def z_target(k):
        return 2 * lax.rem(m + k, mp) + d

    def z_copy(k, other):
        e = 1 - d if other else d
        rows = pl.ds(pl.multiple_of(e * part, part), part)
        device = {"ctx": z_target(k) * nx + x}
        if other:
            device["dp"] = 1 - d
        return remote(
            yr.at[k, rows], zr.at[z], z_send.at[k, int(other)], z_recv.at[z], device
        )

    def scatter_z(k):
        z_copy(k, True).start()

        @pl.when(z_target(k) != z)
        def _():
            z_copy(k, False).start()

        @pl.when(z_target(k) == z)
        def _():
            zr[z] = yr[k, pl.ds(pl.multiple_of(d * part, part), part), :]

    for k in order:
        total = xs[k, x].astype(F32)
        for kx in range(1, nx):
            x_copy(k, kx).wait_recv()
            total = total + xr[k, kx].astype(F32)
        if k:
            ys[k] = total.astype(BF16)
            y_copy(k).start()
        else:
            yr[0] = total.astype(BF16)
            scatter_z(0)
    for k in order:
        if k:
            y_copy(k).wait_recv()
            scatter_z(k)

    ig_copy.wait()
    image_out[:, pl.ds(pl.multiple_of((1 - d) * half, half), half)] = ig_recv[...]

    def wait_z(k, carry):
        @pl.when(jnp.logical_or(k != z, lax.rem(z, 2) != d))
        def _():
            remote(
                yr.at[0, pl.ds(0, part)], zr.at[k], z_send.at[0, 0], z_recv.at[k], {"dp": 1 - d}
            ).wait_recv()

        return carry

    lax.fori_loop(0, nz, wait_z, 0)
    total = zr[0].astype(F32)
    for k in range(1, nz):
        total = total + zr[k].astype(F32)
    wg_send[...] = total
    wg_copy = remote(wg_send, wg_recv, o_sems.at[2], o_sems.at[3], {"dp": 1 - d})
    wg_copy.start()
    weight_out[pl.ds(pl.multiple_of(d * part, part), part), :] = total
    wg_copy.wait()
    weight_out[pl.ds(pl.multiple_of((1 - d) * part, part), part), :] = wg_recv[...]

    for k in order:
        to_partner(k).wait_send()
        for kx in range(1, nx):
            x_copy(k, kx).wait_send()
        if k:
            g_copies[k].wait_send()
            y_copy(k).wait_send()
        z_copy(k, True).wait_send()

        @pl.when(z_target(k) != z)
        def _(k=k):
            z_copy(k, False).wait_send()


def gradients(pos_col, slot_col, prev_grad, own_grad, wh, sht, n, mp):
    half, width = wh.shape[1:]
    tokens = slot_col.shape[0]
    size = own_grad.shape[0]
    nx = n // (2 * mp)
    nz = 2 * mp
    chunk = half // nx
    slots = n * IMGTOK
    vmem = pl.BlockSpec(memory_space=pltpu.VMEM)
    dma = pltpu.SemaphoreType.DMA
    return pl.pallas_call(
        functools.partial(grad_kernel, n, mp, nx, nz),
        out_shape=(
            jax.ShapeDtypeStruct((tokens, 2 * half), BF16),
            jax.ShapeDtypeStruct((chunk, width), F32),
        ),
        in_specs=[vmem] * 6,
        out_specs=(vmem, vmem),
        scratch_shapes=[
            pltpu.VMEM((size, width), BF16),
            pltpu.VMEM((slots, width), BF16),
            pltpu.VMEM((slots, width), BF16),
            pltpu.VMEM((2, mp, tokens, width), BF16),
            pltpu.VMEM((mp, nx, chunk, width), BF16),
            pltpu.VMEM((mp, nx, chunk, width), BF16),
            pltpu.VMEM((mp, chunk, width), BF16),
            pltpu.VMEM((mp, chunk, width), BF16),
            pltpu.VMEM((nz, chunk // 2, width), BF16),
            pltpu.VMEM((chunk // 2, width), F32),
            pltpu.VMEM((chunk // 2, width), F32),
            pltpu.VMEM((tokens, half), BF16),
            pltpu.VMEM((tokens, half), BF16),
            dma((2,)),
            dma((n,)),
            dma((n,)),
            dma((mp,)),
            dma((mp,)),
            dma((mp,)),
            dma((mp,)),
            dma((mp, nx)),
            dma((mp, nx)),
            dma((mp,)),
            dma((mp,)),
            dma((mp, 2)),
            dma((nz,)),
            dma((4,)),
        ],
        compiler_params=pltpu.CompilerParams(
            collective_id=1, has_side_effects=True, vmem_limit_bytes=48 << 20
        ),
        name="gradients",
    )(pos_col, slot_col, prev_grad, own_grad, wh, sht)


def per_device(image_states, place_index, doc_ids, queries, text_kv, kv_weight, d_out):
    n = lax.axis_size("ctx")
    mp = lax.axis_size("mp")
    c = lax.axis_index("ctx")
    size = queries.shape[1]
    tokens = image_states.shape[1]
    hd = kv_weight.shape[2] // 2

    place = place_index[0].reshape(n, tokens)
    own_place = lax.dynamic_slice_in_dim(place, c, 1, axis=0)
    slot_row = (own_place // size) * IMGTOK + own_place % IMGTOK
    local = jnp.where(place // size == c, place % size, -1)
    pos = jnp.max(local.reshape(n, tokens // IMGTOK, IMGTOK), axis=1).reshape(1, n * IMGTOK)

    docs = doc_ids[0].reshape(n, size)
    own_docs = lax.dynamic_slice_in_dim(docs, c, 1, axis=0)
    prior_docs = lax.dynamic_slice_in_dim(docs, jnp.maximum(c - 1, 0), 1, axis=0)
    prior_docs = jnp.where(c > 0, prior_docs, -1)
    key_docs = jnp.concatenate([prior_docs, own_docs], axis=1).reshape(2 * size, 1)

    own_kv, prev_kv, wh, sht = route(
        slot_row, pos, text_kv[0], image_states[0], kv_weight[0], n, mp
    )
    attn_out, prev_grad, own_grad = attention(
        own_docs, key_docs, queries[0], d_out[0], prev_kv, own_kv, hd
    )
    image_grad, weight_grad = gradients(
        pos.reshape(-1, 1), slot_row.reshape(-1, 1), prev_grad, own_grad, wh, sht, n, mp
    )
    return (attn_out[None], image_grad[None], weight_grad[None])


def solution(mesh):
    in_specs = (
        P("dp", "ctx", "mp"),
        P("dp", None),
        P("dp", None),
        P("dp", "ctx", "mp"),
        P("dp", "ctx", "mp"),
        P("mp", None, None),
        P("dp", "ctx", "mp"),
    )
    out_specs = (P("dp", "ctx", "mp"), P("dp", "ctx", "mp"), P("mp", "ctx", None))
    return jax.shard_map(
        per_device, mesh=mesh, in_specs=in_specs, out_specs=out_specs, check_vma=False
    )
```

```python
import functools
import math

import jax
import jax.numpy as jnp
from jax import lax
from jax.experimental import pallas as pl
from jax.experimental.pallas import tpu as pltpu
from jax.sharding import PartitionSpec as P

IMGTOK = 16
BF16 = jnp.bfloat16
F32 = jnp.float32
MESH = pl.DeviceIdType.MESH


def dot_nn(a, b):
    return jnp.dot(a, b, preferred_element_type=F32)


def dot_nt(a, b):
    return lax.dot_general(a, b, (((1,), (1,)), ((), ())), preferred_element_type=F32)


def iota(shape, dim):
    return lax.broadcasted_iota(jnp.int32, shape, dim)


def ring_order(count):
    return sorted(range(count), key=lambda k: (min(k, count - k), k))


def remote(src, dst, send_sem, recv_sem, device):
    return pltpu.make_async_remote_copy(
        src_ref=src,
        dst_ref=dst,
        send_sem=send_sem,
        recv_sem=recv_sem,
        device_id=device,
        device_id_type=MESH,
    )


def slot_exchange(packed, arrived, send_sems, recv_sems, c, n):
    def copy_of(k):
        p = lax.rem(c + k, n)
        return remote(
            packed.at[pl.ds(pl.multiple_of(p * IMGTOK, IMGTOK), IMGTOK)],
            arrived.at[pl.ds(pl.multiple_of(c * IMGTOK, IMGTOK), IMGTOK)],
            send_sems.at[k],
            recv_sems.at[k],
            {"ctx": p},
        )

    def start(k, carry):
        copy_of(k).start()
        return carry

    def finish(k, carry):
        copy_of(k).wait()
        return carry

    lax.fori_loop(1, n, start, 0)
    mine = pl.ds(pl.multiple_of(c * IMGTOK, IMGTOK), IMGTOK)
    arrived[mine, :] = packed[mine, :]
    lax.fori_loop(1, n, finish, 0)


def fused_kernel(
    n,
    mp,
    nx,
    nz,
    hd,
    place_ref,
    docs_ref,
    text_hbm,
    states,
    weights,
    queries,
    grads,
    attn_out,
    image_out,
    weight_out,
    sh,
    wh,
    sht,
    psend,
    precv,
    acc,
    ysend,
    yrecv,
    table,
    pick,
    collect,
    place,
    spread,
    squeeze,
    widen,
    prev_widen,
    prev_squeeze,
    text,
    prev_text,
    packed,
    arrived,
    small,
    small_in,
    q_all,
    g_all,
    out_all,
    bias,
    keys,
    vals,
    vals_t,
    key_sum,
    val_sum,
    small_grad,
    later,
    back,
    gall,
    xs,
    xr,
    ys,
    yr,
    zr,
    wg_send,
    wg_recv,
    ig_send,
    ig_recv,
    local_sems,
    s_sems,
    wa_send,
    wa_recv,
    wb_send,
    wb_recv,
    wc_send,
    wc_recv,
    fx_send,
    fx_recv,
    fz_send,
    fz_recv,
    p_send,
    p_recv,
    i_send,
    i_recv,
    a_send,
    a_recv,
    k_sems,
    b_send,
    b_recv,
    f_send,
    f_recv,
    g_send,
    g_recv,
    x_send,
    x_recv,
    y_send,
    y_recv,
    z_send,
    z_recv,
    o_sems,
):
    c = lax.axis_index("ctx")
    m = lax.axis_index("mp")
    d = lax.axis_index("dp")
    z = c // nx
    x = lax.rem(c, nx)
    order = ring_order(mp)
    tokens, half = sh.shape[1:]
    size = text.shape[0]
    slots = n * IMGTOK
    chunk = half // nx
    part = chunk // 2
    before = lax.rem(c + n - 1, n)

    get_w = pltpu.make_async_copy(
        weights.at[pl.ds(pl.multiple_of(m * 2 * half + d * half, half), half)],
        wh.at[m],
        local_sems.at[0],
    )
    get_s = pltpu.make_async_copy(
        states.at[:, pl.ds(pl.multiple_of(d * half, half), half)], sh.at[d], local_sems.at[1]
    )
    get_text = pltpu.make_async_copy(text_hbm, text, local_sems.at[2])
    get_q = pltpu.make_async_copy(queries, q_all, local_sems.at[3])
    get_g = pltpu.make_async_copy(grads, g_all, local_sems.at[4])
    for copy in (get_w, get_s, get_text, get_q, get_g):
        copy.start()

    barrier = pltpu.get_barrier_semaphore()

    def greet(k, carry):
        pl.semaphore_signal(
            barrier, inc=1, device_id={"ctx": lax.rem(c + k, n)}, device_id_type=MESH
        )
        return carry

    def greet_other(k, carry):
        pl.semaphore_signal(
            barrier,
            inc=1,
            device_id={"dp": 1 - d, "ctx": lax.rem(z + k, nz) * nx + x},
            device_id_type=MESH,
        )
        return carry

    lax.fori_loop(1, n, greet, 0)
    lax.fori_loop(1, nz, greet_other, 0)
    for k in range(1, mp):
        pl.semaphore_signal(
            barrier, inc=1, device_id={"mp": lax.rem(m + k, mp)}, device_id_type=MESH
        )
    pl.semaphore_signal(barrier, inc=1, device_id={"dp": 1 - d}, device_id_type=MESH)
    pl.semaphore_wait(barrier, 1 + (mp - 1) + (n - 1) + (nz - 1))

    rows_a = half // 4
    rows_b = half // 2 // nx
    rows_c = half // 4 // nz
    span_a = pl.ds(0, rows_a)
    first_b = rows_a + x * rows_b
    first_c = rows_a + nx * rows_b + z * rows_c

    def w_copy(k, first, rows, send_sems, recv_sems):
        p = lax.rem(m + k, mp)
        base = p * 2 * half + d * half
        return remote(
            weights.at[pl.ds(pl.multiple_of(base + first, rows), rows)],
            wh.at[m, pl.ds(pl.multiple_of(first, rows), rows)],
            send_sems.at[k],
            recv_sems.at[k],
            {"mp": p},
        )

    far_first = [k for k in reversed(order) if k]
    wc = {k: w_copy(k, first_c, rows_c, wc_send, wc_recv) for k in far_first}
    wb = {k: w_copy(k, first_b, rows_b, wb_send, wb_recv) for k in far_first}
    wa = {k: w_copy(k, 0, rows_a, wa_send, wa_recv) for k in far_first}
    for group in (wc, wb, wa):
        for k in far_first:
            group[k].start()
    s_copy = remote(
        states.at[:, pl.ds(pl.multiple_of((1 - d) * half, half), half)],
        sh.at[d],
        s_sems.at[0],
        s_sems.at[1],
        {"dp": 1 - d},
    )
    s_copy.start()
    get_text.wait()
    text_copy = remote(
        text_hbm, prev_text, k_sems.at[0], k_sems.at[1], {"ctx": lax.rem(c + 1, n)}
    )
    text_copy.start()

    for r in range(n):
        table[r : r + 1, :] = place_ref[:, r * tokens : (r + 1) * tokens]
    own_place = place_ref[:, pl.ds(pl.multiple_of(c * tokens, tokens), tokens)]
    slot_row = lax.div(own_place, size) * IMGTOK + lax.rem(own_place, IMGTOK)
    pick[...] = (iota((slots, tokens), 0) == slot_row).astype(F32).astype(BF16)
    collect[...] = pick[...].T
    fold = (
        (lax.rem(iota((tokens, slots), 0), IMGTOK) == lax.rem(iota((tokens, slots), 1), IMGTOK))
        .astype(F32)
        .astype(BF16)
    )
    earlier = (iota((slots, slots), 0) < iota((slots, slots), 1)).astype(F32).astype(BF16)

    def shard_tables(q):
        marks = jnp.where(
            lax.div(table[...], size) == q, lax.div(lax.rem(table[...], size), IMGTOK) + 1, 0
        )
        sums = dot_nn(marks.astype(F32).astype(BF16), fold)
        of_rank = iota((n, slots), 0) == lax.div(iota((n, slots), 1), IMGTOK)
        row = jnp.sum(jnp.where(of_rank, sums, 0.0), axis=0, keepdims=True)
        valid = row > 0.5
        inside = lax.rem(iota((1, slots), 1), IMGTOK).astype(F32)
        pos = jnp.where(valid, (row - 1.0) * IMGTOK + inside, -1.0)
        to_pos = (iota((size, slots), 0).astype(F32) == pos).astype(F32)
        flags = jnp.broadcast_to(valid.astype(F32), (8, slots)).astype(BF16)
        rank = jnp.where(valid, dot_nn(flags, earlier)[:1], -1.0)
        to_small = (iota((tokens, slots), 0).astype(F32) == rank).astype(F32).astype(BF16)
        return to_pos, to_small

    to_pos, to_small = shard_tables(c)
    is_image = jnp.sum(to_pos, axis=1, keepdims=True) > 0.5
    text[...] = jnp.where(is_image, 0.0, text[...].astype(F32)).astype(BF16)
    place[...] = to_pos.astype(BF16)
    spread[...] = place[...].T
    squeeze[...] = to_small
    widen[...] = dot_nt(place[...], to_small).astype(BF16)
    to_pos, to_small = shard_tables(before)
    is_prev_image = jnp.sum(to_pos, axis=1, keepdims=True) > 0.5
    prev_widen[...] = dot_nt(to_pos.astype(BF16), to_small).astype(BF16)
    prev_squeeze[...] = prev_widen[...].T

    own_docs = docs_ref[:, pl.ds(pl.multiple_of(c * size, size), size)].astype(F32)
    prior_docs = docs_ref[:, pl.ds(pl.multiple_of(before * size, size), size)].astype(F32)
    prior_docs = jnp.where(c > 0, prior_docs, -1.0)
    diagonal = iota((size, size), 0) == iota((size, size), 1)
    block = size // 2
    span = size + block
    own_col = jnp.sum(jnp.where(diagonal, own_docs, 0.0), axis=1, keepdims=True)
    prior_col = jnp.sum(jnp.where(diagonal, prior_docs, 0.0), axis=1, keepdims=True)
    for i in range(2):
        first = i * block
        docs_col = jnp.concatenate([prior_col[first:], own_col[: first + block]], axis=0)
        key_pos = iota((span, block), 0) + (first - size)
        query_pos = iota((span, block), 1) + first
        allowed = (key_pos <= query_pos) & (docs_col == own_docs[:, first : first + block])
        bias[i] = jnp.where(allowed, 0.0, -1e30)
    key_sum[...] = jnp.zeros_like(key_sum)
    val_sum[...] = jnp.zeros_like(val_sum)

    def fx_copy(k, kx):
        rows = pl.ds(pl.multiple_of(first_b, rows_b), rows_b)
        h = lax.rem(m - k + mp, mp)
        return remote(
            wh.at[h, rows],
            wh.at[h, rows],
            fx_send.at[k, kx],
            fx_recv.at[k, kx],
            {"ctx": z * nx + lax.rem(x + kx, nx)},
        )

    def fz_copy(k, kz):
        rows = pl.ds(pl.multiple_of(first_c, rows_c), rows_c)
        h = lax.rem(m - k + mp, mp)
        return remote(
            wh.at[h, rows],
            wh.at[h, rows],
            fz_send.at[k, kz],
            fz_recv.at[k, kz],
            {"ctx": lax.rem(z + kz, nz) * nx + x},
        )

    def each_z(k, action):
        def body(kz, carry):
            action(fz_copy(k, kz))
            return carry

        lax.fori_loop(1, nz, body, 0)

    near_first = [k for k in order if k]
    for k in near_first:
        wc[k].wait_recv()
        each_z(k, lambda copy: copy.start())
        wb[k].wait_recv()
        for kx in range(1, nx):
            fx_copy(k, kx).start()

    get_s.wait()
    get_w.wait()
    s_copy.wait()
    for b in range(2):
        sht[:, b * tokens : (b + 1) * tokens] = sh[b].T
    text_copy.wait()
    prev_text[...] = jnp.where(is_prev_image, 0.0, prev_text[...].astype(F32)).astype(BF16)

    p_copies = {}
    for k in order:
        h = lax.rem(m - k + mp, mp)
        if k:
            wa[k].wait_recv()
            for kx in range(1, nx):
                fx_copy(k, kx).wait_recv()
            each_z(k, lambda copy: copy.wait_recv())
        psend[k] = dot_nn(sh[1 - d], wh[h])
        p_copies[k] = remote(
            psend.at[k], precv.at[k], p_send.at[k], p_recv.at[k], {"dp": 1 - d}
        )
        p_copies[k].start()
        acc[k] = dot_nn(sh[d], wh[h])

    i_copies = {}
    for k in order:
        p_copies[k].wait_recv()
        if k:
            ysend[k] = (acc[k] + precv[k]).astype(BF16)
            i_copies[k] = remote(
                ysend.at[k],
                yrecv.at[k],
                i_send.at[k],
                i_recv.at[k],
                {"mp": lax.rem(m - k + mp, mp)},
            )
            i_copies[k].start()
    total = acc[0] + precv[0]
    for k in near_first:
        i_copies[k].wait_recv()
        total = total + yrecv[k].astype(F32)

    packed[...] = dot_nn(pick[...], total.astype(BF16)).astype(BF16)
    slot_exchange(packed, arrived, a_send, a_recv, c, n)
    small[...] = dot_nn(squeeze[...], arrived[...]).astype(BF16)
    shift = remote(small, small_in, k_sems.at[2], k_sems.at[3], {"ctx": lax.rem(c + 1, n)})
    shift.start()
    own_kv = (dot_nn(place[...], arrived[...]) + text[...].astype(F32)).astype(BF16)
    keys[size:] = own_kv[:, :hd]
    vals[size:] = own_kv[:, hd:]
    get_q.wait()
    get_g.wait()
    shift.wait()
    prev_kv = (dot_nn(prev_widen[...], small_in[...]) + prev_text[...].astype(F32)).astype(BF16)
    keys[:size] = prev_kv[:, :hd]
    vals[:size] = prev_kv[:, hd:]
    vals_t[...] = vals[...].T

    scale = hd ** (-0.5)
    to_log2 = scale / math.log(2.0)

    def one_head(head, carry):
        lanes = pl.ds(pl.multiple_of(head * hd, hd), hd)
        for i in range(2):
            first = i * block
            rows = slice(first, first + block)
            window = slice(first, first + span)
            q = q_all[rows, lanes]
            g = g_all[rows, lanes]
            scores = dot_nt(keys[window, :], q) * to_log2 + bias[i]
            shifted = jnp.exp2(scores - jnp.max(scores, axis=0, keepdims=True))
            probs = shifted * (1.0 / jnp.sum(shifted, axis=0, keepdims=True))
            low = probs.astype(BF16)
            context = dot_nn(vals_t[:, window], low)
            grad_probs = dot_nt(vals[window, :], g)
            delta = jnp.sum(g.T.astype(F32) * context, axis=0, keepdims=True)
            grad_scores = (probs * (grad_probs - delta)).astype(BF16)
            out_all[rows, lanes] = context.T.astype(BF16)
            key_sum[window, :] += dot_nn(grad_scores, q)
            val_sum[window, :] += dot_nn(low, g)
        return carry

    lax.fori_loop(0, q_all.shape[1] // hd, one_head, 0)
    put_out = pltpu.make_async_copy(out_all, attn_out, local_sems.at[5])

    prev_grad = jnp.concatenate(
        [(key_sum[:size] * scale).astype(BF16), val_sum[:size].astype(BF16)], axis=1
    )
    small_grad[...] = dot_nn(prev_squeeze[...], prev_grad).astype(BF16)
    back_shift = remote(small_grad, later, k_sems.at[4], k_sems.at[5], {"ctx": before})
    back_shift.start()
    put_out.start()
    own_grad = jnp.concatenate([key_sum[size:] * scale, val_sum[size:]], axis=1)
    back_shift.wait()
    grad_low = (own_grad + dot_nn(widen[...], later[...])).astype(BF16)
    packed[...] = dot_nn(spread[...], grad_low).astype(BF16)
    slot_exchange(packed, back, b_send, b_recv, c, n)
    gall[d, m] = dot_nn(collect[...], back[...]).astype(BF16)

    def to_partner(k):
        h = lax.rem(m - k + mp, mp)
        return remote(
            gall.at[d, h], gall.at[d, h], f_send.at[k], f_recv.at[k], {"dp": 1 - d}
        )

    g_copies = {}
    to_partner(0).start()
    for k in order:
        if k:
            g_copies[k] = remote(
                gall.at[d, m],
                gall.at[d, m],
                g_send.at[k],
                g_recv.at[k],
                {"mp": lax.rem(m + k, mp)},
            )
            g_copies[k].start()

    def x_copy(k, kx):
        to = lax.rem(x + kx, nx)
        return remote(
            xs.at[k, to], xr.at[k, kx], x_send.at[k, kx], x_recv.at[k, kx], {"ctx": z * nx + to}
        )

    for k in order:
        h = lax.rem(m - k + mp, mp)
        if k:
            g_copies[k].wait_recv()
            to_partner(k).start()
        to_partner(k).wait_recv()
        for j in range(nx):
            rows = slice(j * chunk, (j + 1) * chunk)
            xs[k, j] = (
                dot_nn(sht[rows, :tokens], gall[0, h]) + dot_nn(sht[rows, tokens:], gall[1, h])
            ).astype(BF16)
        for kx in range(1, nx):
            x_copy(k, kx).start()

    ig = dot_nt(gall[1 - d, 0], wh[0])
    for h in range(1, mp):
        ig = ig + dot_nt(gall[1 - d, h], wh[h])
    ig_send[...] = ig.astype(BF16)
    ig_copy = remote(ig_send, ig_recv, o_sems.at[0], o_sems.at[1], {"dp": 1 - d})
    ig_copy.start()
    ig = dot_nt(gall[d, 0], wh[0])
    for h in range(1, mp):
        ig = ig + dot_nt(gall[d, h], wh[h])
    image_out[:, pl.ds(pl.multiple_of(d * half, half), half)] = ig.astype(BF16)

    def y_copy(k):
        return remote(
            ys.at[k], yr.at[k], y_send.at[k], y_recv.at[k], {"mp": lax.rem(m - k + mp, mp)}
        )

    def z_target(k):
        return 2 * lax.rem(m + k, mp) + d

    def z_copy(k, other):
        e = 1 - d if other else d
        rows = pl.ds(pl.multiple_of(e * part, part), part)
        device = {"ctx": z_target(k) * nx + x}
        if other:
            device["dp"] = 1 - d
        return remote(
            yr.at[k, rows], zr.at[z], z_send.at[k, int(other)], z_recv.at[z], device
        )

    def scatter_z(k):
        z_copy(k, True).start()

        @pl.when(z_target(k) != z)
        def _():
            z_copy(k, False).start()

        @pl.when(z_target(k) == z)
        def _():
            zr[z] = yr[k, pl.ds(pl.multiple_of(d * part, part), part), :]

    for k in order:
        total = xs[k, x].astype(F32)
        for kx in range(1, nx):
            x_copy(k, kx).wait_recv()
            total = total + xr[k, kx].astype(F32)
        if k:
            ys[k] = total.astype(BF16)
            y_copy(k).start()
        else:
            yr[0] = total.astype(BF16)
            scatter_z(0)
    for k in order:
        if k:
            y_copy(k).wait_recv()
            scatter_z(k)

    ig_copy.wait()
    image_out[:, pl.ds(pl.multiple_of((1 - d) * half, half), half)] = ig_recv[...]

    def wait_z(k, carry):
        @pl.when(jnp.logical_or(k != z, lax.rem(z, 2) != d))
        def _():
            remote(
                yr.at[0, pl.ds(0, part)], zr.at[k], z_send.at[0, 0], z_recv.at[k], {"dp": 1 - d}
            ).wait_recv()

        return carry

    lax.fori_loop(0, nz, wait_z, 0)
    total = zr[0].astype(F32)
    for k in range(1, nz):
        total = total + zr[k].astype(F32)
    wg_send[...] = total
    wg_copy = remote(wg_send, wg_recv, o_sems.at[2], o_sems.at[3], {"dp": 1 - d})
    wg_copy.start()
    weight_out[pl.ds(pl.multiple_of(d * part, part), part), :] = total
    wg_copy.wait()
    weight_out[pl.ds(pl.multiple_of((1 - d) * part, part), part), :] = wg_recv[...]

    for k in order:
        p_copies[k].wait_send()
        to_partner(k).wait_send()
        for kx in range(1, nx):
            x_copy(k, kx).wait_send()
        if k:
            for group in (wa, wb, wc, i_copies, g_copies):
                group[k].wait_send()
            y_copy(k).wait_send()
            for kx in range(1, nx):
                fx_copy(k, kx).wait_send()
            each_z(k, lambda copy: copy.wait_send())
        z_copy(k, True).wait_send()

        @pl.when(z_target(k) != z)
        def _(k=k):
            z_copy(k, False).wait_send()
    put_out.wait()


def fused(place, docs, text, states, weights, queries, grads, n, mp):
    tokens, slice_width = states.shape
    half = slice_width // 2
    width = weights.shape[1]
    hd = width // 2
    size, heads_width = queries.shape
    block = size // 2
    slots = n * IMGTOK
    nx = n // (2 * mp)
    nz = 2 * mp
    chunk = half // nx
    vmem = pl.BlockSpec(memory_space=pltpu.VMEM)
    hbm = pl.BlockSpec(memory_space=pl.ANY)
    dma = pltpu.SemaphoreType.DMA
    low = lambda *shape: pltpu.VMEM(shape, BF16)
    wide = lambda *shape: pltpu.VMEM(shape, F32)
    return pl.pallas_call(
        functools.partial(fused_kernel, n, mp, nx, nz, hd),
        out_shape=(
            jax.ShapeDtypeStruct((size, heads_width), BF16),
            jax.ShapeDtypeStruct((tokens, slice_width), BF16),
            jax.ShapeDtypeStruct((chunk, width), F32),
        ),
        in_specs=[vmem, vmem, hbm, hbm, hbm, hbm, hbm],
        out_specs=(hbm, vmem, vmem),
        scratch_shapes=[
            low(2, tokens, half),
            low(mp, half, width),
            low(half, 2 * tokens),
            wide(mp, tokens, width),
            wide(mp, tokens, width),
            wide(mp, tokens, width),
            low(mp, tokens, width),
            low(mp, tokens, width),
            pltpu.VMEM((n, tokens), jnp.int32),
            low(slots, tokens),
            low(tokens, slots),
            low(size, slots),
            low(slots, size),
            low(tokens, slots),
            low(size, tokens),
            low(size, tokens),
            low(tokens, size),
            low(size, width),
            low(size, width),
            low(slots, width),
            low(slots, width),
            low(tokens, width),
            low(tokens, width),
            low(size, heads_width),
            low(size, heads_width),
            low(size, heads_width),
            wide(2, size + block, block),
            low(2 * size, hd),
            low(2 * size, hd),
            low(hd, 2 * size),
            wide(2 * size, hd),
            wide(2 * size, hd),
            low(tokens, width),
            low(tokens, width),
            low(slots, width),
            low(2, mp, tokens, width),
            low(mp, nx, chunk, width),
            low(mp, nx, chunk, width),
            low(mp, chunk, width),
            low(mp, chunk, width),
            low(nz, chunk // 2, width),
            wide(chunk // 2, width),
            wide(chunk // 2, width),
            low(tokens, half),
            low(tokens, half),
            dma((6,)),
            dma((2,)),
            *[dma((mp,))] * 6,
            *[dma((mp, nx))] * 2,
            *[dma((mp, nz))] * 2,
            *[dma((mp,))] * 4,
            *[dma((n,))] * 2,
            dma((6,)),
            *[dma((n,))] * 2,
            *[dma((mp,))] * 4,
            *[dma((mp, nx))] * 2,
            *[dma((mp,))] * 2,
            dma((mp, 2)),
            dma((nz,)),
            dma((4,)),
        ],
        compiler_params=pltpu.CompilerParams(
            collective_id=0, has_side_effects=True, vmem_limit_bytes=62 << 20
        ),
        name="fused",
    )(place, docs, text, states, weights, queries, grads)


def per_device(image_states, place_index, doc_ids, queries, text_kv, kv_weight, d_out):
    attn_out, image_grad, weight_grad = fused(
        place_index,
        doc_ids,
        text_kv[0],
        image_states[0],
        kv_weight[0],
        queries[0],
        d_out[0],
        lax.axis_size("ctx"),
        lax.axis_size("mp"),
    )
    return (attn_out[None], image_grad[None], weight_grad[None])


def solution(mesh):
    in_specs = (
        P("dp", "ctx", "mp"),
        P("dp", None),
        P("dp", None),
        P("dp", "ctx", "mp"),
        P("dp", "ctx", "mp"),
        P("mp", None, None),
        P("dp", "ctx", "mp"),
    )
    out_specs = (P("dp", "ctx", "mp"), P("dp", "ctx", "mp"), P("mp", "ctx", None))
    return jax.shard_map(
        per_device, mesh=mesh, in_specs=in_specs, out_specs=out_specs, check_vma=False
    )
```

```python
import functools
import math

import jax
import jax.numpy as jnp
from jax import lax
from jax.experimental import pallas as pl
from jax.experimental.pallas import tpu as pltpu
from jax.sharding import PartitionSpec as P

IMGTOK = 16
BF16 = jnp.bfloat16
F32 = jnp.float32
MESH = pl.DeviceIdType.MESH


def dot_nn(a, b):
    return jnp.dot(a, b, preferred_element_type=F32)


def dot_nt(a, b):
    return lax.dot_general(a, b, (((1,), (1,)), ((), ())), preferred_element_type=F32)


def iota(shape, dim):
    return lax.broadcasted_iota(jnp.int32, shape, dim)


def ring_order(count):
    return sorted(range(count), key=lambda k: (min(k, count - k), k))


def remote(src, dst, send_sem, recv_sem, device):
    return pltpu.make_async_remote_copy(
        src_ref=src,
        dst_ref=dst,
        send_sem=send_sem,
        recv_sem=recv_sem,
        device_id=device,
        device_id_type=MESH,
    )


def slot_exchange(packed, arrived, send_sems, recv_sems, c, n):
    def copy_of(k):
        p = lax.rem(c + k, n)
        return remote(
            packed.at[pl.ds(pl.multiple_of(p * IMGTOK, IMGTOK), IMGTOK)],
            arrived.at[pl.ds(pl.multiple_of(c * IMGTOK, IMGTOK), IMGTOK)],
            send_sems.at[k],
            recv_sems.at[k],
            {"ctx": p},
        )

    def start(k, carry):
        copy_of(k).start()
        return carry

    def finish(k, carry):
        copy_of(k).wait()
        return carry

    lax.fori_loop(1, n, start, 0)
    mine = pl.ds(pl.multiple_of(c * IMGTOK, IMGTOK), IMGTOK)
    arrived[mine, :] = packed[mine, :]
    lax.fori_loop(1, n, finish, 0)


def fused_kernel(
    n,
    mp,
    nx,
    nz,
    hd,
    place_ref,
    docs_ref,
    text_hbm,
    states,
    weights,
    queries,
    grads,
    attn_out,
    image_out,
    weight_out,
    sh,
    wh,
    sht,
    psend,
    precv,
    acc,
    ysend,
    yrecv,
    table,
    pick,
    collect,
    place,
    spread,
    squeeze,
    widen,
    prev_widen,
    prev_squeeze,
    text,
    prev_text,
    packed,
    arrived,
    small,
    small_in,
    q_all,
    g_all,
    out_all,
    bias,
    keys,
    vals,
    vals_t,
    q_stack,
    g_stack,
    low_all,
    ds_all,
    small_grad,
    later,
    back,
    gall,
    xs,
    xa,
    xb,
    yr,
    zr,
    wg_send,
    wg_recv,
    ig_send,
    ig_recv,
    local_sems,
    s_sems,
    wa_send,
    wa_recv,
    wb_send,
    wb_recv,
    wc_send,
    wc_recv,
    fx_send,
    fx_recv,
    fz_send,
    fz_recv,
    p_send,
    p_recv,
    i_send,
    i_recv,
    a_send,
    a_recv,
    k_sems,
    b_send,
    b_recv,
    f_send,
    f_recv,
    g_send,
    g_recv,
    x_send,
    x_recv,
    t_send,
    t_recv,
    z_send,
    z_recv,
    o_sems,
):
    c = lax.axis_index("ctx")
    m = lax.axis_index("mp")
    d = lax.axis_index("dp")
    z = c // nx
    x = lax.rem(c, nx)
    order = ring_order(mp)
    tokens, half = sh.shape[1:]
    size = text.shape[0]
    slots = n * IMGTOK
    chunk = half // nx
    part = chunk // 2
    before = lax.rem(c + n - 1, n)

    pending = []

    get_w = pltpu.make_async_copy(
        weights.at[pl.ds(pl.multiple_of(m * 2 * half + d * half, half), half)],
        wh.at[m],
        local_sems.at[0],
    )
    get_s = pltpu.make_async_copy(
        states.at[:, pl.ds(pl.multiple_of(d * half, half), half)], sh.at[d], local_sems.at[1]
    )
    get_text = pltpu.make_async_copy(text_hbm, text, local_sems.at[2])
    get_q = pltpu.make_async_copy(queries, q_all, local_sems.at[3])
    get_g = pltpu.make_async_copy(grads, g_all, local_sems.at[4])
    for copy in (get_w, get_s, get_text, get_q, get_g):
        copy.start()

    barrier = pltpu.get_barrier_semaphore()

    def greet(k, carry):
        pl.semaphore_signal(
            barrier, inc=1, device_id={"ctx": lax.rem(c + k, n)}, device_id_type=MESH
        )
        return carry

    def greet_other(k, carry):
        pl.semaphore_signal(
            barrier,
            inc=1,
            device_id={"dp": 1 - d, "ctx": lax.rem(z + k, nz) * nx + x},
            device_id_type=MESH,
        )
        return carry

    lax.fori_loop(1, n, greet, 0)
    lax.fori_loop(1, nz, greet_other, 0)
    for k in range(1, mp):
        pl.semaphore_signal(
            barrier, inc=1, device_id={"mp": lax.rem(m + k, mp)}, device_id_type=MESH
        )
    pl.semaphore_signal(barrier, inc=1, device_id={"dp": 1 - d}, device_id_type=MESH)

    for r in range(n):
        table[r : r + 1, :] = place_ref[:, r * tokens : (r + 1) * tokens]
    own_place = place_ref[:, pl.ds(pl.multiple_of(c * tokens, tokens), tokens)]
    slot_row = lax.div(own_place, size) * IMGTOK + lax.rem(own_place, IMGTOK)
    pick[...] = (iota((slots, tokens), 0) == slot_row).astype(F32).astype(BF16)
    collect[...] = pick[...].T
    fold = (
        (lax.rem(iota((tokens, slots), 0), IMGTOK) == lax.rem(iota((tokens, slots), 1), IMGTOK))
        .astype(F32)
        .astype(BF16)
    )
    earlier = (iota((slots, slots), 0) < iota((slots, slots), 1)).astype(F32).astype(BF16)

    def shard_tables(q):
        marks = jnp.where(
            lax.div(table[...], size) == q, lax.div(lax.rem(table[...], size), IMGTOK) + 1, 0
        )
        sums = dot_nn(marks.astype(F32).astype(BF16), fold)
        of_rank = iota((n, slots), 0) == lax.div(iota((n, slots), 1), IMGTOK)
        row = jnp.sum(jnp.where(of_rank, sums, 0.0), axis=0, keepdims=True)
        valid = row > 0.5
        inside = lax.rem(iota((1, slots), 1), IMGTOK).astype(F32)
        pos = jnp.where(valid, (row - 1.0) * IMGTOK + inside, -1.0)
        to_pos = (iota((size, slots), 0).astype(F32) == pos).astype(F32)
        flags = jnp.broadcast_to(valid.astype(F32), (8, slots)).astype(BF16)
        rank = jnp.where(valid, dot_nn(flags, earlier)[:1], -1.0)
        to_small = (iota((tokens, slots), 0).astype(F32) == rank).astype(F32).astype(BF16)
        return to_pos, to_small

    to_pos, to_small = shard_tables(c)
    get_text.wait()
    is_image = jnp.sum(to_pos, axis=1, keepdims=True) > 0.5
    text[...] = jnp.where(is_image, 0.0, text[...].astype(F32)).astype(BF16)
    place[...] = to_pos.astype(BF16)
    spread[...] = place[...].T
    squeeze[...] = to_small
    widen[...] = dot_nt(place[...], to_small).astype(BF16)

    pl.semaphore_wait(barrier, 1 + (mp - 1) + (n - 1) + (nz - 1))

    rows_a = half // 4
    rows_b = half // 2 // nx
    rows_c = half // 4 // nz
    span_a = pl.ds(0, rows_a)
    first_b = rows_a + x * rows_b
    first_c = rows_a + nx * rows_b + z * rows_c

    def w_copy(k, first, rows, send_sems, recv_sems):
        p = lax.rem(m + k, mp)
        base = p * 2 * half + d * half
        return remote(
            weights.at[pl.ds(pl.multiple_of(base + first, rows), rows)],
            wh.at[m, pl.ds(pl.multiple_of(first, rows), rows)],
            send_sems.at[k],
            recv_sems.at[k],
            {"mp": p},
        )

    far_first = [k for k in reversed(order) if k]
    wc = {k: w_copy(k, first_c, rows_c, wc_send, wc_recv) for k in far_first}
    wb = {k: w_copy(k, first_b, rows_b, wb_send, wb_recv) for k in far_first}
    wa = {k: w_copy(k, 0, rows_a, wa_send, wa_recv) for k in far_first}
    for group in (wc, wb, wa):
        for k in far_first:
            group[k].start()
            pending.append(group[k].wait_send)
    s_copy = remote(
        states.at[:, pl.ds(pl.multiple_of((1 - d) * half, half), half)],
        sh.at[d],
        s_sems.at[0],
        s_sems.at[1],
        {"dp": 1 - d},
    )
    s_copy.start()
    text_copy = remote(
        text_hbm, prev_text, k_sems.at[0], k_sems.at[1], {"ctx": lax.rem(c + 1, n)}
    )
    text_copy.start()

    to_pos, to_small = shard_tables(before)
    is_prev_image = jnp.sum(to_pos, axis=1, keepdims=True) > 0.5
    prev_widen[...] = dot_nt(to_pos.astype(BF16), to_small).astype(BF16)
    prev_squeeze[...] = prev_widen[...].T

    def fx_copy(k, kx):
        rows = pl.ds(pl.multiple_of(first_b, rows_b), rows_b)
        h = lax.rem(m - k + mp, mp)
        return remote(
            wh.at[h, rows],
            wh.at[h, rows],
            fx_send.at[k, kx],
            fx_recv.at[k, kx],
            {"ctx": z * nx + lax.rem(x + kx, nx)},
        )

    def fz_copy(k, kz):
        rows = pl.ds(pl.multiple_of(first_c, rows_c), rows_c)
        h = lax.rem(m - k + mp, mp)
        return remote(
            wh.at[h, rows],
            wh.at[h, rows],
            fz_send.at[k, kz],
            fz_recv.at[k, kz],
            {"ctx": lax.rem(z + kz, nz) * nx + x},
        )

    def each_z(k, action):
        def body(kz, carry):
            action(fz_copy(k, kz))
            return carry

        lax.fori_loop(1, nz, body, 0)

    near_first = [k for k in order if k]
    for k in near_first:
        wc[k].wait_recv()
        each_z(k, lambda copy: copy.start())
        pending.append(functools.partial(each_z, k, lambda copy: copy.wait_send()))
        wb[k].wait_recv()
        for kx in range(1, nx):
            fx_copy(k, kx).start()
            pending.append(fx_copy(k, kx).wait_send)


    own_docs = docs_ref[:, pl.ds(pl.multiple_of(c * size, size), size)].astype(F32)
    prior_docs = docs_ref[:, pl.ds(pl.multiple_of(before * size, size), size)].astype(F32)
    prior_docs = jnp.where(c > 0, prior_docs, -1.0)
    diagonal = iota((size, size), 0) == iota((size, size), 1)
    block = size // 2
    span = size + block
    own_col = jnp.sum(jnp.where(diagonal, own_docs, 0.0), axis=1, keepdims=True)
    prior_col = jnp.sum(jnp.where(diagonal, prior_docs, 0.0), axis=1, keepdims=True)
    for i in range(2):
        first = i * block
        docs_col = jnp.concatenate([prior_col[first:], own_col[: first + block]], axis=0)
        key_pos = iota((span, block), 0) + (first - size)
        query_pos = iota((span, block), 1) + first
        allowed = (key_pos <= query_pos) & (docs_col == own_docs[:, first : first + block])
        bias[i] = jnp.where(allowed, 0.0, -1e30)

    get_q.wait()
    get_g.wait()
    heads = q_all.shape[1] // hd
    for i in range(2):
        for head in range(heads):
            rows = slice(i * block, (i + 1) * block)
            lanes = slice(head * hd, (head + 1) * hd)
            q_stack[i, head * block : (head + 1) * block, :] = q_all[rows, lanes]
            g_stack[i, head * block : (head + 1) * block, :] = g_all[rows, lanes]

    get_s.wait()
    get_w.wait()
    s_copy.wait()
    for b in range(2):
        sht[m, :, b * tokens : (b + 1) * tokens] = sh[b].T
    text_copy.wait()
    prev_text[...] = jnp.where(is_prev_image, 0.0, prev_text[...].astype(F32)).astype(BF16)

    p_copies = {}
    for k in order:
        h = lax.rem(m - k + mp, mp)
        if k:
            wa[k].wait_recv()
            for kx in range(1, nx):
                fx_copy(k, kx).wait_recv()
            each_z(k, lambda copy: copy.wait_recv())
        psend[k] = dot_nn(sh[1 - d], wh[h])
        p_copies[k] = remote(
            psend.at[k], precv.at[k], p_send.at[k], p_recv.at[k], {"dp": 1 - d}
        )
        p_copies[k].start()
        pending.append(p_copies[k].wait_send)
        acc[k] = dot_nn(sh[d], wh[h])

    i_copies = {}
    for k in order:
        p_copies[k].wait_recv()
        if k:
            ysend[k] = (acc[k] + precv[k]).astype(BF16)
            i_copies[k] = remote(
                ysend.at[k],
                yrecv.at[k],
                i_send.at[k],
                i_recv.at[k],
                {"mp": lax.rem(m - k + mp, mp)},
            )
            i_copies[k].start()
            pending.append(i_copies[k].wait_send)
    total = acc[0] + precv[0]
    for k in near_first:
        i_copies[k].wait_recv()
        total = total + yrecv[k].astype(F32)

    s_gather = {}
    for k in far_first:
        s_gather[k] = remote(
            sht.at[m], sht.at[m], t_send.at[k], t_recv.at[k], {"mp": lax.rem(m + k, mp)}
        )
        s_gather[k].start()
        pending.append(s_gather[k].wait_send)

    packed[...] = dot_nn(pick[...], total.astype(BF16)).astype(BF16)
    slot_exchange(packed, arrived, a_send, a_recv, c, n)
    small[...] = dot_nn(squeeze[...], arrived[...]).astype(BF16)
    shift = remote(small, small_in, k_sems.at[2], k_sems.at[3], {"ctx": lax.rem(c + 1, n)})
    shift.start()
    own_kv = (dot_nn(place[...], arrived[...]) + text[...].astype(F32)).astype(BF16)
    keys[size:] = own_kv[:, :hd]
    vals[size:] = own_kv[:, hd:]
    shift.wait()
    prev_kv = (dot_nn(prev_widen[...], small_in[...]) + prev_text[...].astype(F32)).astype(BF16)
    keys[:size] = prev_kv[:, :hd]
    vals[:size] = prev_kv[:, hd:]
    vals_t[...] = vals[...].T

    scale = hd ** (-0.5)
    to_log2 = scale / math.log(2.0)

    def one_head(head, carry):
        lanes = pl.ds(pl.multiple_of(head * hd, hd), hd)
        stack = pl.ds(pl.multiple_of(head * block, block), block)
        for i in range(2):
            first = i * block
            window = slice(first, first + span)
            q = q_stack[i, stack, :]
            g = g_stack[i, stack, :]
            scores = dot_nt(keys[window, :], q) * to_log2 + bias[i]
            shifted = jnp.exp2(scores - jnp.max(scores, axis=0, keepdims=True))
            probs = shifted * (1.0 / jnp.sum(shifted, axis=0, keepdims=True))
            low = probs.astype(BF16)
            low_all[i, :, stack] = low
            context = dot_nn(vals_t[:, window], low)
            grad_probs = dot_nt(vals[window, :], g)
            delta = jnp.sum(g.T.astype(F32) * context, axis=0, keepdims=True)
            ds_all[i, :, stack] = (probs * (grad_probs - delta)).astype(BF16)
            out_all[first : first + block, lanes] = context.T.astype(BF16)
        return carry

    lax.fori_loop(0, heads, one_head, 0)
    put_out = pltpu.make_async_copy(out_all, attn_out, local_sems.at[5])

    def prev_sum(left, right):
        both = dot_nn(left[0, :size, :], right[0])
        second = dot_nn(left[1, :block, :], right[1])
        return jnp.concatenate([both[:block], both[block:] + second], axis=0)

    def own_sum(left, right):
        both = dot_nn(left[1, block:, :], right[1])
        second = dot_nn(left[0, size:, :], right[0])
        return jnp.concatenate([both[:block] + second, both[block:]], axis=0)

    prev_grad = jnp.concatenate(
        [prev_sum(ds_all, q_stack) * scale, prev_sum(low_all, g_stack)], axis=1
    ).astype(BF16)
    small_grad[...] = dot_nn(prev_squeeze[...], prev_grad).astype(BF16)
    back_shift = remote(small_grad, later, k_sems.at[4], k_sems.at[5], {"ctx": before})
    back_shift.start()
    put_out.start()
    pending.append(put_out.wait)
    own_grad = jnp.concatenate(
        [own_sum(ds_all, q_stack) * scale, own_sum(low_all, g_stack)], axis=1
    )
    back_shift.wait()
    grad_low = (own_grad + dot_nn(widen[...], later[...])).astype(BF16)
    packed[...] = dot_nn(spread[...], grad_low).astype(BF16)
    slot_exchange(packed, back, b_send, b_recv, c, n)
    gall[d, m] = dot_nn(collect[...], back[...]).astype(BF16)

    def to_partner(k):
        h = lax.rem(m - k + mp, mp)
        return remote(
            gall.at[d, h], gall.at[d, h], f_send.at[k], f_recv.at[k], {"dp": 1 - d}
        )

    g_copies = {}
    to_partner(0).start()
    pending.append(to_partner(0).wait_send)
    for k in order:
        if k:
            g_copies[k] = remote(
                gall.at[d, m],
                gall.at[d, m],
                g_send.at[k],
                g_recv.at[k],
                {"mp": lax.rem(m + k, mp)},
            )
            g_copies[k].start()
            pending.append(g_copies[k].wait_send)

    to_partner(0).wait_recv()
    right, left, opposite = (lax.rem(x + kx, nx) for kx in (1, nx - 1, 2))
    top, bottom = pl.ds(0, part), pl.ds(part, part)

    def x_copy(k, kind):
        to_right = kind % 2 == 0
        near = right if to_right else left
        side = 0 if to_right else 1
        if kind < 2:
            src = xs.at[k, opposite, top if to_right else bottom]
            dst = xa.at[k, side]
        else:
            rows = top if (kind < 4) != to_right else bottom
            src = xs.at[k, near, rows]
            dst = xb.at[k, side, rows]
        return remote(
            src, dst, x_send.at[k, kind], x_recv.at[k, kind], {"ctx": z * nx + near}
        )

    def start_x(k, kinds):
        for kind in kinds:
            x_copy(k, kind).start()
            pending.append(x_copy(k, kind).wait_send)

    def partial_terms(k):
        if k:
            s_gather[k].wait_recv()
        s = lax.rem(m - k + mp, mp)
        both = jnp.concatenate([gall[0, m], gall[1, m]], axis=0)
        for j in range(nx):
            xs[k, j] = dot_nn(sht[s, j * chunk : (j + 1) * chunk, :], both).astype(BF16)
        if nx > 1:
            start_x(k, (0, 1, 2, 3))

    def pass_on(k):
        if nx > 1:
            x_copy(k, 0).wait_recv()
            term = xs[k, right, :part, :].astype(F32) + xa[k, 0].astype(F32)
            xs[k, right, :part, :] = term.astype(BF16)
            start_x(k, (4,))
            x_copy(k, 1).wait_recv()
            term = xs[k, left, part:, :].astype(F32) + xa[k, 1].astype(F32)
            xs[k, left, part:, :] = term.astype(BF16)
            start_x(k, (5,))

    def to_z(k):
        total = xs[k, x].astype(F32)
        if nx > 1:
            for kind in (2, 3, 4, 5):
                x_copy(k, kind).wait_recv()
            total = total + xb[k, 0].astype(F32) + xb[k, 1].astype(F32)
        yr[k] = total.astype(BF16)
        scatter_z(k)

    def z_target(k):
        return 2 * lax.rem(m - k + mp, mp) + d

    def z_copy(k, other):
        e = 1 - d if other else d
        rows = pl.ds(pl.multiple_of(e * part, part), part)
        device = {"ctx": z_target(k) * nx + x}
        if other:
            device["dp"] = 1 - d
        return remote(
            yr.at[k, rows], zr.at[z], z_send.at[k, int(other)], z_recv.at[z], device
        )

    def scatter_z(k):
        z_copy(k, True).start()
        pending.append(z_copy(k, True).wait_send)

        @pl.when(z_target(k) != z)
        def _():
            z_copy(k, False).start()

        def finish():
            @pl.when(z_target(k) != z)
            def _():
                z_copy(k, False).wait_send()

        pending.append(finish)

        @pl.when(z_target(k) == z)
        def _():
            zr[z] = yr[k, pl.ds(pl.multiple_of(d * part, part), part), :]

    for i, k in enumerate(order):
        partial_terms(k)
        if i >= 1:
            pass_on(order[i - 1])
        if i >= 2:
            to_z(order[i - 2])
    pass_on(order[-1])
    for k in near_first:
        g_copies[k].wait_recv()
        to_partner(k).start()
        pending.append(to_partner(k).wait_send)
    if mp > 1:
        to_z(order[-2])
    for k in near_first:
        to_partner(k).wait_recv()
    ig = dot_nt(gall[1 - d, 0], wh[0])
    for h in range(1, mp):
        ig = ig + dot_nt(gall[1 - d, h], wh[h])
    ig_send[...] = ig.astype(BF16)
    ig_copy = remote(ig_send, ig_recv, o_sems.at[0], o_sems.at[1], {"dp": 1 - d})
    ig_copy.start()
    ig = dot_nt(gall[d, 0], wh[0])
    for h in range(1, mp):
        ig = ig + dot_nt(gall[d, h], wh[h])
    image_out[:, pl.ds(pl.multiple_of(d * half, half), half)] = ig.astype(BF16)
    to_z(order[-1])

    ig_copy.wait()
    image_out[:, pl.ds(pl.multiple_of((1 - d) * half, half), half)] = ig_recv[...]

    def wait_z(k, carry):
        @pl.when(jnp.logical_or(k != z, lax.rem(z, 2) != d))
        def _():
            remote(
                yr.at[0, pl.ds(0, part)], zr.at[k], z_send.at[0, 0], z_recv.at[k], {"dp": 1 - d}
            ).wait_recv()

        return carry

    lax.fori_loop(0, nz, wait_z, 0)
    total = zr[0].astype(F32)
    for k in range(1, nz):
        total = total + zr[k].astype(F32)
    wg_send[...] = total
    wg_copy = remote(wg_send, wg_recv, o_sems.at[2], o_sems.at[3], {"dp": 1 - d})
    wg_copy.start()
    weight_out[pl.ds(pl.multiple_of(d * part, part), part), :] = total
    wg_copy.wait()
    weight_out[pl.ds(pl.multiple_of((1 - d) * part, part), part), :] = wg_recv[...]

    for finish in pending:
        finish()


def fused(place, docs, text, states, weights, queries, grads, n, mp):
    tokens, slice_width = states.shape
    half = slice_width // 2
    width = weights.shape[1]
    hd = width // 2
    size, heads_width = queries.shape
    block = size // 2
    slots = n * IMGTOK
    nx = n // (2 * mp)
    nz = 2 * mp
    chunk = half // nx
    vmem = pl.BlockSpec(memory_space=pltpu.VMEM)
    hbm = pl.BlockSpec(memory_space=pltpu.HBM)
    dma = pltpu.SemaphoreType.DMA
    low = lambda *shape: pltpu.VMEM(shape, BF16)
    wide = lambda *shape: pltpu.VMEM(shape, F32)
    return pl.pallas_call(
        functools.partial(fused_kernel, n, mp, nx, nz, hd),
        out_shape=(
            jax.ShapeDtypeStruct((size, heads_width), BF16),
            jax.ShapeDtypeStruct((tokens, slice_width), BF16),
            jax.ShapeDtypeStruct((chunk, width), F32),
        ),
        in_specs=[vmem, vmem, hbm, hbm, hbm, hbm, hbm],
        out_specs=(pl.BlockSpec(memory_space=pl.ANY), vmem, vmem),
        scratch_shapes=[
            low(2, tokens, half),
            low(mp, half, width),
            low(mp, half, 2 * tokens),
            wide(mp, tokens, width),
            wide(mp, tokens, width),
            wide(mp, tokens, width),
            low(mp, tokens, width),
            low(mp, tokens, width),
            pltpu.VMEM((n, tokens), jnp.int32),
            low(slots, tokens),
            low(tokens, slots),
            low(size, slots),
            low(slots, size),
            low(tokens, slots),
            low(size, tokens),
            low(size, tokens),
            low(tokens, size),
            low(size, width),
            low(size, width),
            low(slots, width),
            low(slots, width),
            low(tokens, width),
            low(tokens, width),
            low(size, heads_width),
            low(size, heads_width),
            low(size, heads_width),
            wide(2, size + block, block),
            low(2 * size, hd),
            low(2 * size, hd),
            low(hd, 2 * size),
            low(2, heads_width // hd * block, hd),
            low(2, heads_width // hd * block, hd),
            low(2, size + block, heads_width // hd * block),
            low(2, size + block, heads_width // hd * block),
            low(tokens, width),
            low(tokens, width),
            low(slots, width),
            low(2, mp, tokens, width),
            low(mp, nx, chunk, width),
            low(mp, 2, chunk // 2, width),
            low(mp, 2, chunk, width),
            low(mp, chunk, width),
            low(nz, chunk // 2, width),
            wide(chunk // 2, width),
            wide(chunk // 2, width),
            low(tokens, half),
            low(tokens, half),
            dma((6,)),
            dma((2,)),
            *[dma((mp,))] * 6,
            *[dma((mp, nx))] * 2,
            *[dma((mp, nz))] * 2,
            *[dma((mp,))] * 4,
            *[dma((n,))] * 2,
            dma((6,)),
            *[dma((n,))] * 2,
            *[dma((mp,))] * 4,
            *[dma((mp, 6))] * 2,
            *[dma((mp,))] * 2,
            dma((mp, 2)),
            dma((nz,)),
            dma((4,)),
        ],
        compiler_params=pltpu.CompilerParams(
            collective_id=0, has_side_effects=True, vmem_limit_bytes=47 << 20
        ),
        name="fused",
    )(
        place,
        docs,
        *(
            pltpu.with_memory_space_constraint(a, pltpu.HBM)
            for a in (text, states, weights, queries, grads)
        ),
    )


def per_device(image_states, place_index, doc_ids, queries, text_kv, kv_weight, d_out):
    attn_out, image_grad, weight_grad = fused(
        place_index,
        doc_ids,
        text_kv[0],
        image_states[0],
        kv_weight[0],
        queries[0],
        d_out[0],
        lax.axis_size("ctx"),
        lax.axis_size("mp"),
    )
    return (attn_out[None], image_grad[None], weight_grad[None])


def solution(mesh):
    in_specs = (
        P("dp", "ctx", "mp"),
        P("dp", None),
        P("dp", None),
        P("dp", "ctx", "mp"),
        P("dp", "ctx", "mp"),
        P("mp", None, None),
        P("dp", "ctx", "mp"),
    )
    out_specs = (P("dp", "ctx", "mp"), P("dp", "ctx", "mp"), P("mp", "ctx", None))
    return jax.shard_map(
        per_device, mesh=mesh, in_specs=in_specs, out_specs=out_specs, check_vma=False
    )
```
